32 devices in a mesh: rows: 8 (over y, x, core), cols: 4 (over z).
Axes of the slice: x: 2, y: 2, z: 4, core: 2. Of those that a mesh axis runs over, the one named last changes fastest.
Arguments:
- grads: bfloat16 [2048, 4096], P('rows', 'cols'), may hold values from -6 to 6
- probe: bfloat16 [2048, 4096], P('rows', 'cols'), may hold values from -6 to 6
- left_factor: float32 [2048], P('rows'), may hold values from 0.5 to 2
- q_right: float32 [4096, 4096], P('cols', 'rows'), may hold values from -1 to 2
- q_inv_t: float32 [4096, 4096], P('cols', 'rows'), may hold values from -1 to 2
Outputs:
- left_new: float32 [2048], P('rows')
- q_new: float32 [4096, 4096], P('cols', 'rows')
The draws below stay inside these ranges and needn't reach their ends.
All inputs are finite; a program needn't handle non-finite values. Where the reference program divides by a largest or mean magnitude, that divisor is 1e-20 or more.
Results may differ from the reference program's by a relative error of at most 0.0058.
Values may be sent and summed in bfloat16 or wider, within the bound.
A program may use at most 64 MiB of HBM per device.

```python
import math
import jax
import jax.numpy as jnp
from jax import lax

D = 4096
VOCAB = 2048


def factor_draw(key, salt):
    noise = jax.random.normal(jax.random.fold_in(key, salt), (D, D), jnp.float32)
    noise = jnp.clip(noise, -6.0, 6.0)
    return jnp.eye(D, dtype=jnp.float32) + 0.5 * noise / jnp.sqrt(jnp.float32(D))


def draw_q_right(key, part):
    return factor_draw(key, 11)


def draw_q_inv_t(key, part):
    return factor_draw(key, 23)


def shard_levels(own_key, shape, cuts, least, top_value):
    loudness, own = 1.0, jax.random.fold_in(own_key, 6)
    for position, parts in cuts:
        steps = jnp.exp(jax.random.uniform(jax.random.fold_in(own, position), (parts,), jnp.float32, least / len(cuts), top_value / len(cuts)))
        loudness = loudness * jnp.repeat(steps, shape[position] // parts).reshape([-1 if axis == position else 1 for axis in range(len(shape))])
    return loudness


def centred(key, extent, scale, bound, shards=(), held_as=jnp.bfloat16):
    array = jax.random.normal(key, extent, jnp.float32) * scale
    if len(shards) > 0:
        array = shard_levels(key, extent, shards, -0.22, 0.18) * array
    return jnp.clip(array, min=-bound, max=bound).astype(held_as)


def setup_inputs(seed: int = 0) -> dict:
    key_list = jax.random.split(jax.random.key(seed), 6)
    return {
        "grads": centred(key_list[0], (VOCAB, D), 1.0, 6.0, ((0, 8), (1, 4))),
        "probe": centred(key_list[1], (VOCAB, D), 1.0, 6.0, ((0, 8), (1, 4))),
        "left_factor": jnp.clip(jnp.exp(math.log(2.0) - 1.3862944 * jax.random.uniform(key_list[2], (VOCAB,), jnp.float32) ** shard_levels(key_list[2], (VOCAB,), ((0, 8),), -0.2, 0.2)), 0.5, 2.0),
        "q_right": draw_q_right(jax.random.fold_in(key_list[5], 71), 0),
        "q_inv_t": draw_q_inv_t(jax.random.fold_in(key_list[5], 71), 0),
    }


learn_rate = 0.2
epsilon = 1e-6


def reference(grads, probe, left_factor, q_right, q_inv_t):
    q_low = q_right.astype(jnp.bfloat16)
    inv_low = q_inv_t.astype(jnp.bfloat16)
    white = (left_factor[:, None] * jnp.dot(grads, q_low.T, preferred_element_type=jnp.float32)).astype(jnp.bfloat16)
    conj = ((1.0 / left_factor)[:, None] * jnp.dot(probe, inv_low.T, preferred_element_type=jnp.float32)).astype(jnp.bfloat16)
    white_f = white.astype(jnp.float32)
    conj_f = conj.astype(jnp.float32)
    left_grad = jnp.sum(white_f * white_f - conj_f * conj_f, axis=1)
    gram = jnp.dot(white.T, white, preferred_element_type=jnp.float32) - jnp.dot(conj.T, conj, preferred_element_type=jnp.float32)
    scale_r = learn_rate / (jnp.max(jnp.abs(gram)) + epsilon)
    scale_l = learn_rate / (jnp.max(jnp.abs(left_grad)) + epsilon)
    left_new = left_factor - scale_l * left_grad * left_factor
    q_new = q_right - scale_r * jnp.dot(gram, q_right, precision=lax.Precision.HIGHEST)
    return left_new, q_new
```

```python
import jax
import jax.numpy as jnp
from jax import lax
from jax.sharding import PartitionSpec as P

learn_rate = 0.2
epsilon = 1e-06


def times_t(left, right):
    return lax.dot_general(
        left, right, (((1,), (1,)), ((), ())), preferred_element_type=jnp.float32
    )


def inner_rows(left, right):
    return lax.dot_general(
        left, right, (((0,), (0,)), ((), ())), preferred_element_type=jnp.float32
    )


def shifted(x):
    cols = lax.axis_size("cols")
    return [x] + [
        lax.ppermute(x, "cols", [(c, (c + s) % cols) for c in range(cols)])
        for s in range(1, cols)
    ]


def by_column(pieces):
    cols = len(pieces)
    width = pieces[0].shape[1]
    me = lax.axis_index("cols")
    whole = jnp.zeros((pieces[0].shape[0], cols * width), pieces[0].dtype)
    for s, piece in enumerate(pieces):
        at = lax.rem(me - s + cols, cols) * width
        whole = lax.dynamic_update_slice_in_dim(whole, piece, at, 1)
    return whole


def body(grads, probe, left_factor, q_right, q_inv_t):
    rows = lax.axis_size("rows")
    grad_parts = shifted(grads)
    probe_parts = shifted(probe)
    q_low = q_right.astype(jnp.bfloat16)
    inv_low = q_inv_t.astype(jnp.bfloat16)
    q_rows = lax.all_gather(q_low, "rows", axis=1, tiled=True)
    inv_rows = lax.all_gather(inv_low, "rows", axis=1, tiled=True)
    white_own = (left_factor[:, None] * times_t(by_column(grad_parts), q_rows)).astype(jnp.bfloat16)
    white_parts = shifted(white_own)
    white_all = lax.all_gather(white_own, "rows", axis=0, tiled=True)
    conj_own = ((1.0 / left_factor)[:, None] * times_t(by_column(probe_parts), inv_rows)).astype(jnp.bfloat16)
    conj_parts = shifted(conj_own)
    conj_all = lax.all_gather(conj_own, "rows", axis=0, tiled=True)

    def squares(parts):
        return sum(jnp.sum(jnp.square(p.astype(jnp.float32)), axis=1) for p in parts)

    left_grad = squares(white_parts) - squares(conj_parts)

    def pairs(parts, whole):
        own = lax.all_to_all(jnp.stack(parts), "rows", split_axis=2, concat_axis=1, tiled=True)
        return lax.dot_general(
            own, whole, (((1,), (0,)), ((), ())), preferred_element_type=jnp.float32
        )

    gram_block = pairs(white_parts, white_all) - pairs(conj_parts, conj_all)
    gram_low = gram_block.astype(jnp.bfloat16)
    gram_all = lax.all_gather(gram_low, "rows", axis=0)
    top_r, top_l = lax.pmax(
        (jnp.max(jnp.abs(gram_block)), jnp.max(jnp.abs(left_grad))), ("rows", "cols")
    )
    scale_r = learn_rate / (top_r + epsilon)
    scale_l = learn_rate / (top_l + epsilon)
    left_new = left_factor - scale_l * left_grad * left_factor
    q_blocks = jnp.stack(
        [p.reshape(rows, -1, p.shape[1]) for p in shifted(q_low)], axis=1
    )
    depth = gram_all.shape[0] * gram_all.shape[1] * gram_all.shape[2]
    product = inner_rows(
        gram_all.reshape(depth, -1), q_blocks.reshape(depth, -1)
    )
    q_new = q_right - scale_r * product
    return (left_new, q_new)


def solution(mesh):
    return jax.shard_map(
        body,
        mesh=mesh,
        in_specs=(
            P("rows", "cols"),
            P("rows", "cols"),
            P("rows"),
            P("cols", "rows"),
            P("cols", "rows"),
        ),
        out_specs=(P("rows"), P("cols", "rows")),
        check_vma=False,
    )
```

```python
import jax
import jax.numpy as jnp
from jax import lax
from jax.sharding import PartitionSpec as P


learn_rate = 0.2
epsilon = 1e-06


def shifted(x):
    cols = lax.axis_size("cols")
    return [x] + [
        lax.ppermute(x, "cols", [(c, (c + s) % cols) for c in range(cols)])
        for s in range(1, cols)
    ]


def after(x, earlier):
    return lax.optimization_barrier((x, earlier))[0]


def gather_halves(x):
    rows = lax.axis_size("rows")
    own = lax.all_gather(
        x, "rows", axis=0,
        axis_index_groups=[list(range(0, rows, 2)), list(range(1, rows, 2))],
    )
    return own, lax.ppermute(own, "rows", [(r, r ^ 1) for r in range(rows)])


def parities():
    core = lax.rem(lax.axis_index("rows"), 2)
    return core, 1 - core


def by_column(pieces):
    cols, rows = len(pieces), lax.axis_size("rows")
    me = lax.axis_index("cols")
    pairs = rows // cols // 2
    height, width = pieces[0].shape
    width = width * cols // rows
    halves = []
    for parity in parities():
        whole = jnp.zeros((rows // 2, height, width), pieces[0].dtype)
        for s, piece in enumerate(pieces):
            first = lax.rem(me - s + cols, cols) * pairs
            for t in range(pairs):
                block = lax.dynamic_slice_in_dim(piece, (2 * t + parity) * width, width, 1)
                whole = lax.dynamic_update_slice_in_dim(whole, block[None], first + t, 0)
        halves.append(whole)
    return halves


def dot_blocks(left, right, left_dims, right_dims):
    return lax.dot_general(
        left, right, ((left_dims, right_dims), ((), ())),
        preferred_element_type=jnp.float32,
    )


def body(grads, probe, left_factor, q_right, q_inv_t):
    rows = lax.axis_size("rows")

    def rotate(parts, factor_halves, gain):
        total = 0.0
        for x, f in zip(by_column(parts), factor_halves):
            total += dot_blocks(x, f, (0, 2), (0, 2))
        return (gain[:, None] * total).astype(jnp.bfloat16)

    probe_parts = shifted(probe)
    inv_halves = gather_halves(q_inv_t.astype(jnp.bfloat16))
    grad_parts = shifted(after(grads, probe_parts))
    q_low = q_right.astype(jnp.bfloat16)
    q_halves = gather_halves(q_low)
    conj_own = rotate(probe_parts, inv_halves, 1.0 / left_factor)
    conj_parts = shifted(conj_own)
    white_own = rotate(grad_parts, q_halves, left_factor)
    white_parts = shifted(white_own)
    q_parts = shifted(after(q_low, (conj_parts, white_parts)))
    conj_halves = gather_halves(conj_own)
    white_halves = gather_halves(white_own)

    def squares(parts):
        return sum(jnp.sum(jnp.square(p.astype(jnp.float32)), axis=1) for p in parts)

    left_grad = squares(white_parts) - squares(conj_parts)

    def pairs(parts, halves):
        own = lax.all_to_all(jnp.stack(parts), "rows", split_axis=2, concat_axis=1, tiled=True)
        own = own.reshape(own.shape[0], rows // 2, 2, -1, own.shape[2])
        total = 0.0
        for parity, half in zip(parities(), halves):
            mine = lax.dynamic_index_in_dim(own, parity, 2, keepdims=False)
            total += dot_blocks(mine, half, (1, 2), (0, 1))
        return total

    gram_block = pairs(conj_parts, conj_halves)
    gram_block = pairs(white_parts, white_halves) - gram_block
    gram_halves = gather_halves(gram_block.astype(jnp.bfloat16))
    top_r, top_l = lax.pmax(
        (jnp.max(jnp.abs(gram_block)), jnp.max(jnp.abs(left_grad))), ("rows", "cols")
    )
    scale_r = learn_rate / (top_r + epsilon)
    scale_l = learn_rate / (top_l + epsilon)
    left_new = left_factor - scale_l * left_grad * left_factor
    product = 0.0
    for parity, half in zip(parities(), gram_halves):
        blocks = [
            lax.dynamic_index_in_dim(
                p.reshape(rows // 2, 2, -1, p.shape[1]), parity, 1, keepdims=False
            )
            for p in q_parts
        ]
        product += dot_blocks(half, jnp.stack(blocks, axis=1), (0, 1, 2), (0, 1, 2))
    q_new = q_right - scale_r * product
    return (left_new, q_new)


def solution(mesh):
    return jax.shard_map(
        body,
        mesh=mesh,
        in_specs=(
            P("rows", "cols"),
            P("rows", "cols"),
            P("rows"),
            P("cols", "rows"),
            P("cols", "rows"),
        ),
        out_specs=(P("rows"), P("cols", "rows")),
        check_vma=False,
    )
```

```python
import jax
import jax.numpy as jnp
from jax import lax
from jax.sharding import PartitionSpec as P


learn_rate = 0.2
epsilon = 1e-06


def shifted(x):
    cols = lax.axis_size("cols")
    return [x] + [
        lax.ppermute(x, "cols", [(c, (c + s) % cols) for c in range(cols)])
        for s in range(1, cols)
    ]


def after(x, earlier):
    return lax.optimization_barrier((x, earlier))[0]


def gather_halves(x):
    rows = lax.axis_size("rows")
    pair = lax.axis_index("rows") // 2
    own = jnp.zeros((rows // 2, *x.shape), x.dtype)
    for d in range(rows // 2):
        part = x
        if d > 0:
            part = lax.ppermute(x, "rows", [(r, r ^ (2 * d)) for r in range(rows)])
        own = lax.dynamic_update_slice_in_dim(own, part[None], lax.bitwise_xor(pair, d), 0)
    return own, lax.ppermute(own, "rows", [(r, r ^ 1) for r in range(rows)])


def parities():
    core = lax.rem(lax.axis_index("rows"), 2)
    return core, 1 - core


def by_column(pieces):
    cols, rows = len(pieces), lax.axis_size("rows")
    me = lax.axis_index("cols")
    pairs = rows // cols // 2
    height, width = pieces[0].shape
    width = width * cols // rows
    halves = []
    for parity in parities():
        whole = jnp.zeros((rows // 2, height, width), pieces[0].dtype)
        for s, piece in enumerate(pieces):
            first = lax.rem(me - s + cols, cols) * pairs
            for t in range(pairs):
                block = lax.dynamic_slice_in_dim(piece, (2 * t + parity) * width, width, 1)
                whole = lax.dynamic_update_slice_in_dim(whole, block[None], first + t, 0)
        halves.append(whole)
    return halves


def dot_blocks(left, right, left_dims, right_dims):
    return lax.dot_general(
        left, right, ((left_dims, right_dims), ((), ())),
        preferred_element_type=jnp.float32,
    )


def body(grads, probe, left_factor, q_right, q_inv_t):
    rows = lax.axis_size("rows")

    def rotate(parts, factor_halves, gain):
        total = 0.0
        for x, f in zip(by_column(parts), factor_halves):
            total += dot_blocks(x, f, (0, 2), (0, 2))
        return (gain[:, None] * total).astype(jnp.bfloat16)

    probe_parts = shifted(probe)
    inv_halves = gather_halves(q_inv_t.astype(jnp.bfloat16))
    grad_parts = shifted(after(grads, probe_parts))
    q_low = q_right.astype(jnp.bfloat16)
    q_halves = gather_halves(after(q_low, inv_halves[0]))
    conj_own = rotate(probe_parts, inv_halves, 1.0 / left_factor)
    conj_parts = shifted(conj_own)
    white_own = rotate(grad_parts, q_halves, left_factor)
    conj_parts = after(conj_parts, white_own)
    white_parts = shifted(white_own)
    q_parts = shifted(after(q_low, (conj_parts, white_parts)))
    conj_halves = gather_halves(conj_own)
    white_halves = gather_halves(white_own)

    def squares(parts):
        return sum(jnp.sum(jnp.square(p.astype(jnp.float32)), axis=1) for p in parts)

    left_grad = squares(white_parts) - squares(conj_parts)

    def pairs(parts, halves):
        own = lax.all_to_all(jnp.stack(parts), "rows", split_axis=2, concat_axis=1, tiled=True)
        own = own.reshape(own.shape[0], rows // 2, 2, -1, own.shape[2])
        total = 0.0
        for parity, half in zip(parities(), halves):
            mine = lax.dynamic_index_in_dim(own, parity, 2, keepdims=False)
            total += dot_blocks(mine, half, (1, 2), (0, 1))
        return total

    gram_block = pairs(conj_parts, conj_halves)
    gram_block = pairs(white_parts, white_halves) - gram_block
    gram_halves = gather_halves(gram_block.astype(jnp.bfloat16))
    top_r, top_l = lax.pmax(
        (jnp.max(jnp.abs(gram_block)), jnp.max(jnp.abs(left_grad))), ("rows", "cols")
    )
    scale_r = learn_rate / (top_r + epsilon)
    scale_l = learn_rate / (top_l + epsilon)
    left_new = left_factor - scale_l * left_grad * left_factor
    product = 0.0
    for parity, half in zip(parities(), gram_halves):
        blocks = [
            lax.dynamic_index_in_dim(
                p.reshape(rows // 2, 2, -1, p.shape[1]), parity, 1, keepdims=False
            )
            for p in q_parts
        ]
        product += dot_blocks(half, jnp.stack(blocks, axis=1), (0, 1, 2), (0, 1, 2))
    q_new = q_right - scale_r * product
    return (left_new, q_new)


def solution(mesh):
    return jax.shard_map(
        body,
        mesh=mesh,
        in_specs=(
            P("rows", "cols"),
            P("rows", "cols"),
            P("rows"),
            P("cols", "rows"),
            P("cols", "rows"),
        ),
        out_specs=(P("rows"), P("cols", "rows")),
        check_vma=False,
    )
```

```python
import jax
import jax.numpy as jnp
from jax import lax
from jax.sharding import PartitionSpec as P


learn_rate = 0.2
epsilon = 1e-06


def times_t(left, right):
    return lax.dot_general(
        left, right, (((1,), (1,)), ((), ())), preferred_element_type=jnp.float32
    )


def inner_rows(left, right):
    return lax.dot_general(
        left, right, (((0,), (0,)), ((), ())), preferred_element_type=jnp.float32
    )


def shifted(x):
    cols = lax.axis_size("cols")
    return [x] + [
        lax.ppermute(x, "cols", [(c, (c + s) % cols) for c in range(cols)])
        for s in range(1, cols)
    ]


def after(x, earlier):
    return lax.optimization_barrier((x, earlier))[0]


def by_column(pieces):
    cols = len(pieces)
    width = pieces[0].shape[1]
    me = lax.axis_index("cols")
    whole = jnp.zeros((pieces[0].shape[0], cols * width), pieces[0].dtype)
    for s, piece in enumerate(pieces):
        at = lax.rem(me - s + cols, cols) * width
        whole = lax.dynamic_update_slice_in_dim(whole, piece, at, 1)
    return whole


def body(grads, probe, left_factor, q_right, q_inv_t):
    rows = lax.axis_size("rows")
    height = grads.shape[0]
    both_parts = shifted(jnp.concatenate([probe, grads]))
    probe_parts = [p[:height] for p in both_parts]
    grad_parts = [p[height:] for p in both_parts]
    q_low = q_right.astype(jnp.bfloat16)
    inv_low = q_inv_t.astype(jnp.bfloat16)
    q_rows = lax.all_gather(q_low, "rows", axis=1, tiled=True)
    inv_rows = lax.all_gather(inv_low, "rows", axis=1, tiled=True)
    conj_own = ((1.0 / left_factor)[:, None] * times_t(by_column(probe_parts), inv_rows)).astype(jnp.bfloat16)
    conj_parts = shifted(conj_own)
    conj_all = lax.all_gather(conj_own, "rows", axis=0, tiled=True)
    q_rows = after(q_rows, conj_parts)
    white_own = (left_factor[:, None] * times_t(by_column(grad_parts), q_rows)).astype(jnp.bfloat16)
    white_parts = shifted(white_own)
    q_parts = shifted(after(q_low, white_parts))
    white_all = lax.all_gather(white_own, "rows", axis=0, tiled=True)

    def squares(parts):
        return sum(jnp.sum(jnp.square(p.astype(jnp.float32)), axis=1) for p in parts)

    left_grad = squares(white_parts) - squares(conj_parts)

    def pairs(parts, whole):
        own = lax.all_to_all(jnp.stack(parts), "rows", split_axis=2, concat_axis=1, tiled=True)
        return lax.dot_general(
            own, whole, (((1,), (0,)), ((), ())), preferred_element_type=jnp.float32
        )

    gram_block = pairs(white_parts, white_all) - pairs(conj_parts, conj_all)
    gram_low = gram_block.astype(jnp.bfloat16)
    gram_all = lax.all_gather(gram_low, "rows", axis=0)
    top_r, top_l = lax.pmax(
        (jnp.max(jnp.abs(gram_block)), jnp.max(jnp.abs(left_grad))), ("rows", "cols")
    )
    scale_r = learn_rate / (top_r + epsilon)
    scale_l = learn_rate / (top_l + epsilon)
    left_new = left_factor - scale_l * left_grad * left_factor
    q_blocks = jnp.stack(
        [p.reshape(rows, -1, p.shape[1]) for p in q_parts], axis=1
    )
    depth = gram_all.shape[0] * gram_all.shape[1] * gram_all.shape[2]
    product = inner_rows(
        gram_all.reshape(depth, -1), q_blocks.reshape(depth, -1)
    )
    q_new = q_right - scale_r * product
    return (left_new, q_new)


def solution(mesh):
    return jax.shard_map(
        body,
        mesh=mesh,
        in_specs=(
            P("rows", "cols"),
            P("rows", "cols"),
            P("rows"),
            P("cols", "rows"),
            P("cols", "rows"),
        ),
        out_specs=(P("rows"), P("cols", "rows")),
        check_vma=False,
    )
```
